32 devices in a mesh: slab: 4 (over y, core), probe: 8 (over z, x).
Axes of the slice: x: 2, y: 2, z: 4, core: 2. Of those that a mesh axis runs over, the one named last changes fastest.
Arguments:
- sources: bfloat16 [64, 64, 16, 512], P('probe', 'slab'), may hold values from -6 to 6
- conductivity: float32 [64, 16, 512], P('slab'), may hold values from 0.1 to 10
- well_mask: int32 [64, 16, 512], P('slab'), may hold values 0 or 1
- zone_map: int32 [64, 16, 512], P('slab'), may hold values from 0 to 1023, as said below
- forward_drive: bfloat16 [64, 16, 512], P('slab'), may hold values from -6 to 6
- group_counts: int32 [8], replicated, may hold values from 0 to 8, as said below
- sketch: float32 [16, 64], replicated, may hold values from -0.75 to 0.75
Outputs:
- basis: float32 [1024, 16], P(('slab', 'probe'))
- factor: float32 [16, 16], replicated
The draws below stay inside these ranges and needn't reach their ends.
Inputs may be any that keep to these rules, and one draw needn't show every extreme that they name: `group_counts`: groups g and g + 4 have counts that add up to 8; some group has 8. `zone_map`: A cell at x lies in a zone (x // 8 * 2 + bz) * 64 + by, where bz and by differ from the cell's own z and y blocks by at most one; every zone holds cells.
All inputs are finite; a program needn't handle non-finite values. No bound on the sum of `well_mask` on one device may be relied on, other than what follows from the above.
Results may differ from the reference program's by a relative error of at most 0.0003.
Values may be sent and summed in bfloat16 or wider, within the bound.
A program may use at most 128 MiB of HBM per device.

```python
import math
import jax
import jax.numpy as jnp
from jax import lax

NY = 512
NZ = 16
ZB = 8
FLD_DEV = 8
SWEEPS = 3
NX = 64
FIELDS = 64
GROUPS = 8
RANK = 16
ZONES = 1024


def draw_zone_map(key, part):
    key_z, key_y = jax.random.split(jax.random.fold_in(key, 11), 2)
    shape = (NX, NZ, NY)
    xpos = lax.broadcasted_iota(jnp.int32, shape, 0)
    zpos = lax.broadcasted_iota(jnp.int32, shape, 1)
    ypos = lax.broadcasted_iota(jnp.int32, shape, 2)
    flip_z = jax.random.randint(key_z, shape, 0, 2)
    flip_y = jax.random.randint(key_y, shape, 0, 2)
    shift_z = jnp.where((zpos % ZB == 0) & (flip_z == 1), -1, 0) + jnp.where((zpos % ZB == ZB - 1) & (flip_z == 1), 1, 0)
    shift_y = jnp.where((ypos % ZB == 0) & (flip_y == 1), -1, 0) + jnp.where((ypos % ZB == ZB - 1) & (flip_y == 1), 1, 0)
    block_z = jnp.clip(zpos // ZB + shift_z, 0, NZ // ZB - 1)
    block_y = jnp.clip(ypos // ZB + shift_y, 0, NY // ZB - 1)
    return ((xpos // ZB * (NZ // ZB) + block_z) * (NY // ZB) + block_y).astype(jnp.int32)


def draw_group_counts(key, part):
    key_low, key_pick = jax.random.split(jax.random.fold_in(key, 23), 2)
    paired = GROUPS // 2
    lower = jax.random.randint(key_low, (paired,), 0, FLD_DEV + 1)
    chosen = jax.random.randint(key_pick, (), 0, paired)
    lower = jnp.where(jnp.arange(paired) == chosen, FLD_DEV, lower)
    return jnp.concatenate([lower, FLD_DEV - lower]).astype(jnp.int32)


def with_ends(array, own_key, low, largest):
    longest = array.shape.index(max(array.shape))
    spots = []
    for shift in (0, 1):
        where = [jax.random.randint(jax.random.fold_in(own_key, axis), (), 0, length) for axis, length in enumerate(array.shape)]
        where[longest] = (where[longest] + shift) % array.shape[longest]
        spots.append(tuple(where))
    return array.at[spots[0]].set(low).at[spots[1]].set(largest)


def block_levels(key, shape, shards, smallest, high):
    def one(axis_at, shards_of):
        heights = jax.random.uniform(jax.random.fold_in(jax.random.fold_in(key, 6), axis_at), (shards_of,), jnp.float32, smallest / len(shards), high / len(shards))
        return jnp.repeat(jnp.exp(heights), shape[axis_at] // shards_of).reshape((-1,) + (1,) * (len(shape) - axis_at - 1))

    gain = one(*shards[0])
    for cut in shards[1:]:
        gain = gain * one(*cut)
    return gain


def bell_draw(key, shape, scale, most, pieces=(), kind=jnp.bfloat16):
    entries = jax.random.normal(key, shape, jnp.float32) * scale
    if len(pieces) > 0:
        entries = block_levels(key, shape, pieces, -0.22, 0.18) * entries
    return jnp.clip(entries, min=-most, max=most).astype(kind)


def setup_inputs(seed: int = 0) -> dict:
    streams_of = jax.random.split(jax.random.key(seed), 8)
    return {
        "sources": bell_draw(streams_of[0], (FIELDS, NX, NZ, NY), 1.0, 6.0, ((0, 8), (1, 4))),
        "conductivity": jnp.clip(jnp.exp(math.log(10.0) - 4.6051702 * jax.random.uniform(streams_of[1], (NX, NZ, NY), jnp.float32) ** block_levels(streams_of[1], (NX, NZ, NY), ((0, 4),), -0.2, 0.2)), 0.1, 10.0),
        "well_mask": with_ends((jax.random.randint(streams_of[2], (NX, NZ, NY), 0, 8) < 1).astype(jnp.int32), jax.random.fold_in(streams_of[2], 1), 0, 1),
        "zone_map": draw_zone_map(jax.random.fold_in(streams_of[7], 71), 0),
        "forward_drive": bell_draw(streams_of[4], (NX, NZ, NY), 1.0, 6.0, ((0, 4),)),
        "group_counts": draw_group_counts(jax.random.fold_in(streams_of[7], 71), 0),
        "sketch": bell_draw(streams_of[6], (RANK, FIELDS), FIELDS ** -0.5, 0.75, (), jnp.float32),
    }


storage_term = 0.2
well_conductance = 4.0
spectrum_low = 0.1
spectrum_high = 2.0

def harmonic(left, right):
    return 2.0 * left * right / (left + right)

def apply_operator(value, face_x, face_z, face_y, diagonal_sum):
    padded = jnp.pad(value, 1)
    beside = face_x[1:] * padded[2:, 1:-1, 1:-1] + face_x[:-1] * padded[:-2, 1:-1, 1:-1]
    beside = beside + face_z[:, 1:] * padded[1:-1, 2:, 1:-1] + face_z[:, :-1] * padded[1:-1, :-2, 1:-1]
    beside = beside + face_y[:, :, 1:] * padded[1:-1, 1:-1, 2:] + face_y[:, :, :-1] * padded[1:-1, 1:-1, :-2]
    return diagonal_sum * value - beside

def reference(sources, conductivity, well_mask, zone_map, forward_drive, group_counts, sketch):
    cond_padded = jnp.pad(conductivity, 1)
    face_x = harmonic(cond_padded[:-1, 1:-1, 1:-1], cond_padded[1:, 1:-1, 1:-1])
    face_z = harmonic(cond_padded[1:-1, :-1, 1:-1], cond_padded[1:-1, 1:, 1:-1])
    face_y = harmonic(cond_padded[1:-1, 1:-1, :-1], cond_padded[1:-1, 1:-1, 1:])
    diagonal_sum = face_x[1:] + face_x[:-1] + face_z[:, 1:] + face_z[:, :-1] + face_y[:, :, 1:] + face_y[:, :, :-1]
    diagonal_sum = diagonal_sum + storage_term + well_conductance * well_mask.astype(jnp.float32)
    inverse = 1.0 / diagonal_sum
    drive = forward_drive.astype(jnp.float32)
    field_index = jnp.arange(FIELDS, dtype=jnp.int32)
    active = (field_index % FLD_DEV < group_counts[field_index // FLD_DEV]).astype(jnp.float32)
    zone_flat = zone_map.reshape(-1).astype(jnp.int32)
    middle = (spectrum_high + spectrum_low) / 2.0
    radius = (spectrum_high - spectrum_low) / 2.0
    aspect = middle / radius
    zone_scale = float(ZB) ** (-1.5)

    def one_field(item):
        source, switch = item
        forcing = source.astype(jnp.float32) * switch
        remain = forcing
        update = inverse * remain / middle
        head = jnp.zeros_like(forcing)
        rho_prev = 1.0 / aspect
        for sweep in range(SWEEPS):
            head = head + update
            remain = remain - apply_operator(update, face_x, face_z, face_y, diagonal_sum)
            rho_new = 1.0 / (2.0 * aspect - rho_prev)
            update = rho_new * rho_prev * update + 2.0 * rho_new / radius * inverse * remain
            rho_prev = rho_new
        head = head + update
        sensitivity = (head * drive).reshape(-1)
        return jax.ops.segment_sum(sensitivity, zone_flat, num_segments=ZONES) * zone_scale
    gradients = lax.map(one_field, (sources, active))
    sketched = jnp.dot(sketch, gradients, precision=lax.Precision.HIGHEST)
    panel = sketched.T
    orthonormal, upper = jnp.linalg.qr(panel)
    signs = jnp.sign(jnp.diagonal(upper))
    root = math.sqrt(ZONES)
    basis = orthonormal * signs[None, :] * root
    factor = upper * signs[:, None] / root
    return (basis, factor)
```

```python
import functools
import math

import jax
import jax.numpy as jnp
from jax import lax
from jax.experimental import pallas as pl
from jax.experimental.pallas import tpu as pltpu
from jax.sharding import PartitionSpec as P

ZB = 8
SWEEPS = 3
PAIR = 2

storage_term = 0.2
well_conductance = 4.0
spectrum_low = 0.1
spectrum_high = 2.0

MESH = pl.DeviceIdType.MESH
VMEM = pltpu.VMEM
HIGH = lax.Precision.HIGHEST


def head_polynomial():
    middle = (spectrum_high + spectrum_low) / 2.0
    radius = (spectrum_high - spectrum_low) / 2.0
    aspect = middle / radius
    size = SWEEPS + 1
    update = [1.0] + [0.0] * SWEEPS
    remain = [middle] + [0.0] * SWEEPS
    head = [0.0] * size
    rho_prev = 1.0 / aspect
    for sweep in range(SWEEPS):
        head = [h + u for h, u in zip(head, update)]
        moved = [0.0] + update[:-1]
        remain = [r - u + m for r, u, m in zip(remain, update, moved)]
        rho_new = 1.0 / (2.0 * aspect - rho_prev)
        update = [rho_new * rho_prev * u + 2.0 * rho_new / radius * r for u, r in zip(update, remain)]
        rho_prev = rho_new
    head = [h + u for h, u in zip(head, update)]
    return head, middle


def harmonic(left, right):
    total = left + right
    return 2.0 * left * right / jnp.where(total > 0, total, 1.0)


def sweep_kernel(rows, src, slo, shi, cond, mlo, mhi, well, zone, drive, out,
                 cext, wext, inv, gxp, gxm, gzp, gzm, gyp, gym, md, v0, ha, hb, red):
    fields, cells, nz, ny = src.shape
    rim = SWEEPS
    ext = cells + 2 * rim
    nbz, nby = nz // ZB, ny // ZB
    poly, middle = head_polynomial()
    ratio = [p / poly[-1] for p in poly]
    yid = lax.broadcasted_iota(jnp.int32, (nz, ny), 1)
    zid = lax.broadcasted_iota(jnp.int32, (nz, ny), 0)

    cext[0:rim + 1] = mlo[0:rim + 1]
    cext[rim + 1:rim + 1 + cells] = cond[...]
    cext[rim + 1 + cells:] = mhi[0:rim + 1]
    wext[0:rim] = mlo[rim + 1:]
    wext[rim:rim + cells] = well[...].astype(jnp.float32)
    wext[rim + cells:] = mhi[rim + 1:]

    def media(e, carry):
        below, fxm = carry
        c = below
        above = cext[e + 2]
        fxp = harmonic(c, above)
        fyp = jnp.where(yid < ny - 1, harmonic(c, pltpu.roll(c, ny - 1, 1)), 0.0)
        fym = pltpu.roll(fyp, 1, 1)
        fzp = jnp.where(zid < nz - 1, harmonic(c, pltpu.roll(c, nz - 1, 0)), 0.0)
        fzm = pltpu.roll(fzp, 1, 0)
        diagonal_sum = fxp + fxm + fzp + fzm + fyp + fym
        diagonal_sum = diagonal_sum + storage_term + well_conductance * wext[e]
        inverse = 1.0 / diagonal_sum
        inv[e] = inverse * (poly[-1] / middle)
        gxp[e] = fxp * inverse
        gxm[e] = fxm * inverse
        gzp[e] = fzp * inverse
        gzm[e] = fzm * inverse
        gyp[e] = fyp * inverse
        gym[e] = fym * inverse
        return above, fxp

    lax.fori_loop(0, ext, media, (cext[1], harmonic(cext[0], cext[1])))

    slab = lax.axis_index("slab")
    scale = float(ZB) ** (-1.5)

    @pl.loop(0, cells)
    def _(x):
        block = (slab * cells + x) // ZB
        rel = zone[x] - block * (nbz * nby) - yid // ZB
        weight = drive[x].astype(jnp.float32) * scale
        for bz in range(nbz):
            for dy in range(3):
                md[x, bz * 3 + dy] = jnp.where(rel == bz * nby + dy - 1, weight, 0.0)

    @pl.loop(0, fields // PAIR)
    def _(pair):
        first = pair * PAIR
        for j in range(PAIR):
            for e in range(rim):
                v0[j, e] = slo[first + j, e].astype(jnp.float32) * inv[e]
                far = rim + cells + e
                v0[j, far] = shi[first + j, e].astype(jnp.float32) * inv[far]

        @pl.loop(0, cells)
        def _(x):
            own = inv[x + rim]
            for j in range(PAIR):
                v0[j, x + rim] = src[first + j, x].astype(jnp.float32) * own

        value = v0
        for sweep in range(SWEEPS):
            target = ha if sweep % 2 == 0 else hb
            factor = ratio[SWEEPS - 1 - sweep]

            def step(e, unused, value=value, target=target, factor=factor):
                for j in range(PAIR):
                    mid = value[j, e]
                    total = factor * v0[j, e]
                    total = total + gxp[e] * value[j, e + 1] + gxm[e] * value[j, e - 1]
                    total = total + gzp[e] * pltpu.roll(mid, nz - 1, 0) + gzm[e] * pltpu.roll(mid, 1, 0)
                    total = total + gyp[e] * pltpu.roll(mid, ny - 1, 1) + gym[e] * pltpu.roll(mid, 1, 1)
                    target[j, e] = total
                return unused

            lax.fori_loop(sweep + 1, ext - sweep - 1, step, 0)
            value = target

        for j in range(PAIR):
            for xb in range(cells // ZB):
                def gather(x, sums, j=j, xb=xb, value=value):
                    plane = xb * ZB + x
                    head = value[j, plane + rim]
                    grown = []
                    for k in range(nbz * 3):
                        part = head * md[plane, k]
                        both = part[0:ZB]
                        for half in range(1, nbz):
                            both = both + part[half * ZB:(half + 1) * ZB]
                        grown.append(sums[k] + both)
                    return tuple(grown)

                zero = jnp.zeros((ZB, ny), jnp.float32)
                sums = lax.fori_loop(0, ZB, gather, (zero,) * (nbz * 3))
                for k in range(nbz * 3):
                    red[xb, k, pl.ds(first + j, 1)] = jnp.sum(sums[k], axis=0, keepdims=True)

    ypos = lax.broadcasted_iota(jnp.int32, (ny, nby), 0) // ZB
    bpos = lax.broadcasted_iota(jnp.int32, (ny, nby), 1)
    table = jnp.concatenate([(ypos + dy - 1 == bpos).astype(jnp.float32) for dy in range(3)], axis=0)
    per = nby // rows
    for xb in range(cells // ZB):
        for bz in range(nbz):
            wide = jnp.concatenate([red[xb, bz * 3 + dy] for dy in range(3)], axis=1)
            grad = jnp.dot(wide, table, precision=HIGH, preferred_element_type=jnp.float32)
            for part in range(per):
                out[(xb * nbz + bz) * per + part] = grad[:, part * rows:(part + 1) * rows]


def tail_kernel(root, slabs, groups, pieces, chosen, basis, factor,
                landed, mine, grams, send_a, recv_a, send_b, recv_b):
    rank = chosen.shape[1]
    fields, rows = pieces.shape[1:]
    slab = lax.axis_index("slab")
    group = lax.axis_index("probe")
    count = slabs * groups
    me = slab * groups + group

    barrier = pltpu.get_barrier_semaphore()

    def greet(d, unused):
        other = lax.rem(me + d, count)
        pl.semaphore_signal(barrier, inc=1, device_id=(other // groups, lax.rem(other, groups)), device_id_type=MESH)
        return unused

    lax.fori_loop(1, count, greet, 0)
    pl.semaphore_wait(barrier, count - 1)

    def piece_copy(d):
        to = lax.rem(group + d, groups)
        return pltpu.make_async_remote_copy(
            src_ref=pieces.at[to], dst_ref=landed.at[d], send_sem=send_a.at[d], recv_sem=recv_a.at[d],
            device_id=(slab, to), device_id_type=MESH)

    for d in range(1, groups):
        piece_copy(d).start()
    landed[0] = pieces[group]
    for d in range(1, groups):
        piece_copy(d).wait()

    panel = jnp.zeros((rank, rows), jnp.float32)
    for d in range(groups):
        owner = lax.rem(group + groups - d, groups)
        panel = panel + jnp.dot(chosen[owner], landed[d], precision=HIGH, preferred_element_type=jnp.float32)
    gram = lax.dot_general(panel, panel, (((1,), (1,)), ((), ())), precision=HIGH,
                           preferred_element_type=jnp.float32)
    mine[...] = gram

    def gram_copy(d):
        to = lax.rem(me + d, count)
        return pltpu.make_async_remote_copy(
            src_ref=mine, dst_ref=grams.at[me], send_sem=send_b.at[d], recv_sem=recv_b.at[d],
            device_id=(to // groups, lax.rem(to, groups)), device_id_type=MESH)

    def start(d, unused):
        gram_copy(d).start()
        return unused

    def finish(d, unused):
        gram_copy(d).wait()
        return unused

    lax.fori_loop(1, count, start, 0)
    grams[me] = gram
    lax.fori_loop(1, count, finish, 0)
    upper = jnp.sum(grams[...], axis=0)

    rid = lax.broadcasted_iota(jnp.int32, (rank, 1), 0)
    right = panel
    for j in range(rank):
        grow = 1.0 / jnp.sqrt(upper[j:j + 1, j:j + 1])
        row = upper[j:j + 1, :] * grow
        row_right = right[j:j + 1, :] * grow
        column = jnp.where(rid > j, upper[:, j:j + 1] * grow, 0.0)
        upper = jnp.where(rid == j, row, upper - column * row)
        right = jnp.where(rid == j, row_right, right - column * row_right)
    cid = lax.broadcasted_iota(jnp.int32, (rank, rank), 1)
    factor[...] = jnp.where(cid >= rid, upper, 0.0) / root
    basis[...] = right * root


def halo(cells, axis, width, dim):
    count = lax.axis_size(axis)
    ends = count - 1
    head = lax.slice_in_dim(cells, 0, width, axis=dim)
    tail = lax.slice_in_dim(cells, cells.shape[dim] - width, cells.shape[dim], axis=dim)
    low = lax.ppermute(tail, axis, [(i, i + 1) for i in range(ends)])
    high = lax.ppermute(head, axis, [(i + 1, i) for i in range(ends)])
    return low, high


def shards(sources, conductivity, well_mask, zone_map, forward_drive, group_counts, sketch):
    fields, cells, nz, ny = sources.shape
    groups = lax.axis_size("probe")
    slabs = lax.axis_size("slab")
    rank = sketch.shape[0]
    rim = SWEEPS
    ext = cells + 2 * rim
    nbz, nby = nz // ZB, ny // ZB
    zone_count = cells // ZB * nbz * nby
    rows = zone_count // groups

    slo, shi = halo(sources, "slab", rim, 1)
    clo, chi = halo(conductivity, "slab", rim + 1, 0)
    wlo, whi = halo(well_mask.astype(jnp.float32), "slab", rim, 0)
    mlo = jnp.concatenate([clo, wlo], axis=0)
    mhi = jnp.concatenate([chi, whi], axis=0)

    slots = jnp.arange(fields, dtype=jnp.int32)
    active = (slots[None, :] < group_counts[:, None]).astype(jnp.float32)
    chosen = jnp.moveaxis(sketch.reshape(rank, groups, fields) * active[None], 1, 0)

    vmem = pl.BlockSpec(memory_space=VMEM)
    plane = (nz, ny)
    f32 = jnp.float32
    pieces = pl.pallas_call(
        functools.partial(sweep_kernel, rows),
        out_shape=jax.ShapeDtypeStruct((groups, fields, rows), f32),
        in_specs=[vmem] * 9,
        out_specs=vmem,
        scratch_shapes=[
            VMEM((ext + 2,) + plane, f32),
            VMEM((ext,) + plane, f32),
        ] + [VMEM((ext,) + plane, f32)] * 7 + [
            VMEM((cells, nbz * 3) + plane, f32),
            VMEM((PAIR, ext) + plane, f32),
            VMEM((PAIR, ext) + plane, f32),
            VMEM((PAIR, ext) + plane, f32),
            VMEM((cells // ZB, nbz * 3, fields, ny), f32),
        ],
        compiler_params=pltpu.CompilerParams(vmem_limit_bytes=48 << 20),
        name="sweeps",
    )(sources, slo, shi, conductivity, mlo, mhi, well_mask, zone_map, forward_drive)

    root = math.sqrt(zone_count * slabs)
    dma = pltpu.SemaphoreType.DMA
    count = slabs * groups
    basis, factor = pl.pallas_call(
        functools.partial(tail_kernel, root, slabs, groups),
        out_shape=(jax.ShapeDtypeStruct((rank, rows), f32), jax.ShapeDtypeStruct((rank, rank), f32)),
        in_specs=[vmem] * 2,
        out_specs=(vmem, vmem),
        scratch_shapes=[
            VMEM((groups, fields, rows), f32),
            VMEM((rank, rank), f32),
            VMEM((count, rank, rank), f32),
            dma((groups,)), dma((groups,)), dma((count,)), dma((count,)),
        ],
        compiler_params=pltpu.CompilerParams(collective_id=0, has_side_effects=True),
        name="tail",
    )(pieces, chosen)
    return basis.T, factor


def solution(mesh):
    in_specs = (
        P("probe", "slab", None, None),
        P("slab", None, None),
        P("slab", None, None),
        P("slab", None, None),
        P("slab", None, None),
        P(),
        P(),
    )
    out_specs = (P(("slab", "probe"), None), P())
    return jax.shard_map(shards, mesh=mesh, in_specs=in_specs, out_specs=out_specs, check_vma=False)
```

```python
import functools
import math

import jax
import jax.numpy as jnp
from jax import lax
from jax.experimental import pallas as pl
from jax.experimental.pallas import tpu as pltpu
from jax.sharding import PartitionSpec as P

ZB = 8
SWEEPS = 3
PAIR = 2

storage_term = 0.2
well_conductance = 4.0
spectrum_low = 0.1
spectrum_high = 2.0

MESH = pl.DeviceIdType.MESH
VMEM = pltpu.VMEM
HIGH = lax.Precision.HIGHEST


def head_polynomial():
    middle = (spectrum_high + spectrum_low) / 2.0
    radius = (spectrum_high - spectrum_low) / 2.0
    aspect = middle / radius
    size = SWEEPS + 1
    update = [1.0] + [0.0] * SWEEPS
    remain = [middle] + [0.0] * SWEEPS
    head = [0.0] * size
    rho_prev = 1.0 / aspect
    for sweep in range(SWEEPS):
        head = [h + u for h, u in zip(head, update)]
        moved = [0.0] + update[:-1]
        remain = [r - u + m for r, u, m in zip(remain, update, moved)]
        rho_new = 1.0 / (2.0 * aspect - rho_prev)
        update = [rho_new * rho_prev * u + 2.0 * rho_new / radius * r for u, r in zip(update, remain)]
        rho_prev = rho_new
    head = [h + u for h, u in zip(head, update)]
    return head, middle


def harmonic(left, right):
    total = left + right
    return 2.0 * left * right / jnp.where(total > 0, total, 1.0)


def whole_kernel(root, slabs, groups, src, cond, well, zone, drive, counts, sketch, basis, factor,
                 slo, shi, cext, wext, inv, gxp, gxm, gzp, gzm, gyp, gym, md, v0, ha, hb, red,
                 pieces, landed, mine, grams, send_h, recv_h, send_a, recv_a, send_b, recv_b):
    fields, cells, nz, ny = src.shape
    rank = sketch.shape[0]
    rows = pieces.shape[2]
    rim = SWEEPS
    ext = cells + 2 * rim
    nbz, nby = nz // ZB, ny // ZB
    poly, middle = head_polynomial()
    ratio = [p / poly[-1] for p in poly]
    yid = lax.broadcasted_iota(jnp.int32, (nz, ny), 1)
    zid = lax.broadcasted_iota(jnp.int32, (nz, ny), 0)

    slab = lax.axis_index("slab")
    group = lax.axis_index("probe")
    me = slab * groups + group
    slab_at = [slab] + [lax.rem(slab + d, slabs) for d in range(1, slabs)]
    group_at = [group] + [lax.rem(group + d, groups) for d in range(1, groups)]
    others = [(s, g) for s in range(slabs) for g in range(groups) if s + g > 0]

    barrier = pltpu.get_barrier_semaphore()
    for s, g in others:
        pl.semaphore_signal(barrier, inc=1, device_id=(slab_at[s], group_at[g]), device_id_type=MESH)

    cext[rim + 1:rim + 1 + cells] = cond[...]
    wext[rim:rim + cells] = well[...]
    scale = float(ZB) ** (-1.5)

    @pl.loop(0, cells)
    def _(x):
        block = (slab * cells + x) // ZB
        rel = zone[x] - block * (nbz * nby) - yid // ZB
        weight = drive[x].astype(jnp.float32) * scale
        for bz in range(nbz):
            for dy in range(3):
                md[x, bz * 3 + dy] = jnp.where(rel == bz * nby + dy - 1, weight, 0.0)

    pl.semaphore_wait(barrier, len(others))

    def rim_copies(side):
        if side == 0:
            to = slab_at[1]
            parts = (
                (cond.at[pl.ds(cells - rim - 1, rim + 1)], cext.at[pl.ds(0, rim + 1)]),
                (well.at[pl.ds(cells - rim, rim)], wext.at[pl.ds(0, rim)]),
                (src.at[:, pl.ds(cells - rim, rim)], slo),
            )
        else:
            to = slab_at[slabs - 1]
            parts = (
                (cond.at[pl.ds(0, rim + 1)], cext.at[pl.ds(rim + 1 + cells, rim + 1)]),
                (well.at[pl.ds(0, rim)], wext.at[pl.ds(rim + cells, rim)]),
                (src.at[:, pl.ds(0, rim)], shi),
            )
        return [
            pltpu.make_async_remote_copy(
                src_ref=here, dst_ref=there, send_sem=send_h.at[side, k], recv_sem=recv_h.at[side, k],
                device_id=(to, group), device_id_type=MESH)
            for k, (here, there) in enumerate(parts)
        ]

    has_next, has_prev = slab < slabs - 1, slab > 0

    @pl.when(has_next)
    def _():
        for copy in rim_copies(0):
            copy.start()

    @pl.when(has_prev)
    def _():
        for copy in rim_copies(1):
            copy.start()

    @pl.when(slab == 0)
    def _():
        cext[0:rim + 1] = jnp.zeros((rim + 1, nz, ny), jnp.float32)
        wext[0:rim] = jnp.zeros((rim, nz, ny), jnp.int32)
        slo[...] = jnp.zeros_like(slo)

    @pl.when(slab == slabs - 1)
    def _():
        cext[rim + 1 + cells:] = jnp.zeros((rim + 1, nz, ny), jnp.float32)
        wext[rim + cells:] = jnp.zeros((rim, nz, ny), jnp.int32)
        shi[...] = jnp.zeros_like(shi)

    def media(e, carry):
        c, fxm = carry
        above = cext[e + 2]
        fxp = harmonic(c, above)
        fyp = jnp.where(yid < ny - 1, harmonic(c, pltpu.roll(c, ny - 1, 1)), 0.0)
        fym = pltpu.roll(fyp, 1, 1)
        fzp = jnp.where(zid < nz - 1, harmonic(c, pltpu.roll(c, nz - 1, 0)), 0.0)
        fzm = pltpu.roll(fzp, 1, 0)
        diagonal_sum = fxp + fxm + fzp + fzm + fyp + fym
        diagonal_sum = diagonal_sum + storage_term + well_conductance * wext[e].astype(jnp.float32)
        inverse = 1.0 / diagonal_sum
        inv[e] = inverse * (poly[-1] / middle)
        gxp[e] = fxp * inverse
        gxm[e] = fxm * inverse
        gzp[e] = fzp * inverse
        gzm[e] = fzm * inverse
        gyp[e] = fyp * inverse
        gym[e] = fym * inverse
        return above, fxp

    def media_planes(low, high):
        lax.fori_loop(low, high, media, (cext[low + 1], harmonic(cext[low], cext[low + 1])))

    media_planes(rim + 1, rim + cells - 1)

    @pl.when(has_prev)
    def _():
        for copy in rim_copies(0):
            copy.wait_recv()

    @pl.when(has_next)
    def _():
        for copy in rim_copies(1):
            copy.wait_recv()

    media_planes(0, rim + 1)
    media_planes(rim + cells - 1, ext)

    @pl.loop(0, fields // PAIR)
    def _(pair):
        first = pair * PAIR

        def rim_start(e, unused):
            far = rim + cells + e
            for j in range(PAIR):
                v0[j, e] = slo[first + j, e].astype(jnp.float32) * inv[e]
                v0[j, far] = shi[first + j, e].astype(jnp.float32) * inv[far]
            return unused

        def own_start(x, unused):
            own = inv[x + rim]
            for j in range(PAIR):
                v0[j, x + rim] = src[first + j, x].astype(jnp.float32) * own
            return unused

        lax.fori_loop(0, rim, rim_start, 0)
        lax.fori_loop(0, cells, own_start, 0)

        value = v0
        for sweep in range(SWEEPS):
            target = ha if sweep % 2 == 0 else hb
            weight = ratio[SWEEPS - 1 - sweep]

            def step(e, unused, value=value, target=target, weight=weight):
                for j in range(PAIR):
                    mid = value[j, e]
                    total = weight * v0[j, e]
                    total = total + gxp[e] * value[j, e + 1] + gxm[e] * value[j, e - 1]
                    total = total + gzp[e] * pltpu.roll(mid, nz - 1, 0) + gzm[e] * pltpu.roll(mid, 1, 0)
                    total = total + gyp[e] * pltpu.roll(mid, ny - 1, 1) + gym[e] * pltpu.roll(mid, 1, 1)
                    target[j, e] = total
                return unused

            lax.fori_loop(sweep + 1, ext - sweep - 1, step, 0)
            value = target

        for j in range(PAIR):
            for xb in range(cells // ZB):
                def gather(x, sums, j=j, xb=xb, value=value):
                    plane = xb * ZB + x
                    head = value[j, plane + rim]
                    grown = []
                    for k in range(nbz * 3):
                        part = head * md[plane, k]
                        both = part[0:ZB]
                        for half in range(1, nbz):
                            both = both + part[half * ZB:(half + 1) * ZB]
                        grown.append(sums[k] + both)
                    return tuple(grown)

                zero = jnp.zeros((ZB, ny), jnp.float32)
                sums = lax.fori_loop(0, ZB, gather, (zero,) * (nbz * 3))
                for k in range(nbz * 3):
                    red[xb, k, pl.ds(first + j, 1)] = jnp.sum(sums[k], axis=0, keepdims=True)

    ypos = lax.broadcasted_iota(jnp.int32, (ny, nby), 0) // ZB
    bpos = lax.broadcasted_iota(jnp.int32, (ny, nby), 1)
    table = jnp.concatenate([(ypos + dy - 1 == bpos).astype(jnp.float32) for dy in range(3)], axis=0)
    per = nby // rows
    wide = jnp.concatenate([
        jnp.concatenate([red[xb, bz * 3 + dy] for dy in range(3)], axis=1)
        for xb in range(cells // ZB) for bz in range(nbz)
    ], axis=0)
    grad = jnp.dot(wide, table, precision=HIGH, preferred_element_type=jnp.float32)
    for at in range(groups):
        block, part = at // per, at % per
        pieces[at] = grad[block * fields:(block + 1) * fields, part * rows:(part + 1) * rows]

    @pl.when(has_next)
    def _():
        for copy in rim_copies(0):
            copy.wait_send()

    @pl.when(has_prev)
    def _():
        for copy in rim_copies(1):
            copy.wait_send()

    def piece_copy(d):
        return pltpu.make_async_remote_copy(
            src_ref=pieces.at[group_at[d]], dst_ref=landed.at[group], send_sem=send_a.at[d],
            recv_sem=recv_a.at[d], device_id=(slab, group_at[d]), device_id_type=MESH)

    for d in range(1, groups):
        piece_copy(d).start()
    landed[group] = pieces[group]
    lane = lax.broadcasted_iota(jnp.int32, sketch.shape, 1)
    active = jnp.zeros(sketch.shape, jnp.bool_)
    for g in range(groups):
        start = g * fields
        active = active | ((lane >= start) & (lane < start + counts[g]) & (lane < start + fields))
    chosen = jnp.where(active, sketch[...], 0.0)
    for d in range(1, groups):
        piece_copy(d).wait()

    every = landed[...].reshape(groups * fields, rows)
    panel = jnp.dot(chosen, every, precision=HIGH, preferred_element_type=jnp.float32)
    gram = lax.dot_general(panel, panel, (((1,), (1,)), ((), ())), precision=HIGH,
                           preferred_element_type=jnp.float32)
    mine[...] = gram

    def gram_copy(s, g):
        return pltpu.make_async_remote_copy(
            src_ref=mine, dst_ref=grams.at[me], send_sem=send_b.at[s * groups + g],
            recv_sem=recv_b.at[s * groups + g], device_id=(slab_at[s], group_at[g]), device_id_type=MESH)

    for s, g in others:
        gram_copy(s, g).start()
    grams[me] = gram
    for s, g in others:
        gram_copy(s, g).wait()
    upper = jnp.sum(grams[...], axis=0)

    rid = lax.broadcasted_iota(jnp.int32, (rank, 1), 0)
    right = panel
    for j in range(rank - 1):
        column = jnp.where(rid > j, upper[:, j:j + 1] * (1.0 / upper[j:j + 1, j:j + 1]), 0.0)
        right = right - column * right[j:j + 1, :]
        upper = upper - column * upper[j:j + 1, :]
    full = lax.broadcasted_iota(jnp.int32, (rank, rank), 0)
    cid = lax.broadcasted_iota(jnp.int32, (rank, rank), 1)
    pivots = jnp.sum(jnp.where(cid == full, upper, 0.0), axis=1, keepdims=True)
    grow = 1.0 / jnp.sqrt(pivots)
    factor[...] = jnp.where(cid >= full, upper * grow, 0.0) / root
    basis[...] = right * grow * root


def shards(sources, conductivity, well_mask, zone_map, forward_drive, group_counts, sketch):
    fields, cells, nz, ny = sources.shape
    groups = lax.axis_size("probe")
    slabs = lax.axis_size("slab")
    rank = sketch.shape[0]
    rim = SWEEPS
    ext = cells + 2 * rim
    nbz, nby = nz // ZB, ny // ZB
    zone_count = cells // ZB * nbz * nby
    rows = zone_count // groups
    root = math.sqrt(zone_count * slabs)
    count = slabs * groups
    vmem = pl.BlockSpec(memory_space=VMEM)
    plane = (nz, ny)
    f32 = jnp.float32
    dma = pltpu.SemaphoreType.DMA
    basis, factor = pl.pallas_call(
        functools.partial(whole_kernel, root, slabs, groups),
        out_shape=(jax.ShapeDtypeStruct((rank, rows), f32), jax.ShapeDtypeStruct((rank, rank), f32)),
        in_specs=[vmem] * 5 + [pl.BlockSpec(memory_space=pltpu.SMEM), vmem],
        out_specs=(vmem, vmem),
        scratch_shapes=[
            VMEM((fields, rim) + plane, sources.dtype),
            VMEM((fields, rim) + plane, sources.dtype),
            VMEM((ext + 2,) + plane, f32),
            VMEM((ext,) + plane, jnp.int32),
        ] + [VMEM((ext,) + plane, f32)] * 7 + [
            VMEM((cells, nbz * 3) + plane, f32),
            VMEM((PAIR, ext) + plane, f32),
            VMEM((PAIR, ext) + plane, f32),
            VMEM((PAIR, ext) + plane, f32),
            VMEM((cells // ZB, nbz * 3, fields, ny), f32),
            VMEM((groups, fields, rows), f32),
            VMEM((groups, fields, rows), f32),
            VMEM((rank, rank), f32),
            VMEM((count, rank, rank), f32),
            dma((2, 3)), dma((2, 3)), dma((groups,)), dma((groups,)), dma((count,)), dma((count,)),
        ],
        compiler_params=pltpu.CompilerParams(
            collective_id=0, has_side_effects=True, vmem_limit_bytes=56 << 20),
        name="whole",
    )(sources, conductivity, well_mask, zone_map, forward_drive, group_counts, sketch)
    return basis.T, factor


def solution(mesh):
    in_specs = (
        P("probe", "slab", None, None),
        P("slab", None, None),
        P("slab", None, None),
        P("slab", None, None),
        P("slab", None, None),
        P(),
        P(),
    )
    out_specs = (P(("slab", "probe"), None), P())
    return jax.shard_map(shards, mesh=mesh, in_specs=in_specs, out_specs=out_specs, check_vma=False)
```

```python
import functools
import math

import jax
import jax.numpy as jnp
from jax import lax
from jax.experimental import pallas as pl
from jax.experimental.pallas import tpu as pltpu
from jax.sharding import PartitionSpec as P

ZB = 8
SWEEPS = 3
PAIR = 2
UNROLL = 2
LANES = 128

storage_term = 0.2
well_conductance = 4.0
spectrum_low = 0.1
spectrum_high = 2.0

MESH = pl.DeviceIdType.MESH
VMEM = pltpu.VMEM
HIGH = lax.Precision.HIGHEST


def head_polynomial():
    middle = (spectrum_high + spectrum_low) / 2.0
    radius = (spectrum_high - spectrum_low) / 2.0
    aspect = middle / radius
    size = SWEEPS + 1
    update = [1.0] + [0.0] * SWEEPS
    remain = [middle] + [0.0] * SWEEPS
    head = [0.0] * size
    rho_prev = 1.0 / aspect
    for sweep in range(SWEEPS):
        head = [h + u for h, u in zip(head, update)]
        moved = [0.0] + update[:-1]
        remain = [r - u + m for r, u, m in zip(remain, update, moved)]
        rho_new = 1.0 / (2.0 * aspect - rho_prev)
        update = [rho_new * rho_prev * u + 2.0 * rho_new / radius * r for u, r in zip(update, remain)]
        rho_prev = rho_new
    head = [h + u for h, u in zip(head, update)]
    return head, middle


def harmonic(left, right):
    total = left + right
    return 2.0 * left * right / jnp.where(total > 0, total, 1.0)


def whole_kernel(root, slabs, groups, src, cond, well, zone, drive, counts, sketch, basis, factor,
                 slo, shi, cext, wext, inv, gxp, gxm, gzp, gzm, gyp, gym, md, v0, ha, hb, red,
                 pieces, landed, mine, grams, send_h, recv_h, send_a, recv_a, send_b, recv_b):
    fields, cells, nz, ny = src.shape
    rank = sketch.shape[0]
    rows = pieces.shape[2]
    rim = SWEEPS
    ext = cells + 2 * rim
    nbz, nby = nz // ZB, ny // ZB
    poly, middle = head_polynomial()
    ratio = [p / poly[-1] for p in poly]
    yid = lax.broadcasted_iota(jnp.int32, (nz, ny), 1)
    zid = lax.broadcasted_iota(jnp.int32, (nz, ny), 0)

    slab = lax.axis_index("slab")
    group = lax.axis_index("probe")
    me = slab * groups + group
    slab_at = [slab] + [lax.rem(slab + d, slabs) for d in range(1, slabs)]
    group_at = [group] + [lax.rem(group + d, groups) for d in range(1, groups)]
    others = [(s, g) for s in range(slabs) for g in range(groups) if s + g > 0]

    barrier = pltpu.get_barrier_semaphore()
    for s, g in others:
        pl.semaphore_signal(barrier, inc=1, device_id=(slab_at[s], group_at[g]), device_id_type=MESH)

    cext[rim + 1:rim + 1 + cells] = cond[...]
    wext[rim:rim + cells] = well[...]
    scale = float(ZB) ** (-1.5)

    @pl.loop(0, cells)
    def _(x):
        block = (slab * cells + x) // ZB
        rel = zone[x] - block * (nbz * nby) - yid // ZB
        weight = drive[x].astype(jnp.float32) * scale
        for bz in range(nbz):
            for dy in range(3):
                md[x, bz * 3 + dy] = jnp.where(rel == bz * nby + dy - 1, weight, 0.0)

    tiles = ny // LANES
    inner, above, below = pl.ds(ZB, nz), pl.ds(ZB + 1, nz), pl.ds(ZB - 1, nz)
    lane = lax.broadcasted_iota(jnp.int32, (nz, LANES), 1)

    @pl.loop(0, ext)
    def _(e):
        blank = jnp.zeros((ZB, LANES), jnp.float32)
        for buffer in (v0, ha, hb):
            for j in range(PAIR):
                for t in range(tiles):
                    buffer[j, e, t, 0:ZB] = blank
                    buffer[j, e, t, ZB + nz:] = blank

    pl.semaphore_wait(barrier, len(others))

    def rim_copies(side):
        if side == 0:
            to = slab_at[1]
            parts = (
                (cond.at[pl.ds(cells - rim - 1, rim + 1)], cext.at[pl.ds(0, rim + 1)]),
                (well.at[pl.ds(cells - rim, rim)], wext.at[pl.ds(0, rim)]),
            )
        else:
            to = slab_at[slabs - 1]
            parts = (
                (cond.at[pl.ds(0, rim + 1)], cext.at[pl.ds(rim + 1 + cells, rim + 1)]),
                (well.at[pl.ds(0, rim)], wext.at[pl.ds(rim + cells, rim)]),
            )
        return [
            pltpu.make_async_remote_copy(
                src_ref=here, dst_ref=there, send_sem=send_h.at[side, k], recv_sem=recv_h.at[side, k],
                device_id=(to, group), device_id_type=MESH)
            for k, (here, there) in enumerate(parts)
        ]

    def source_copy(side, pair):
        some = pl.ds(pair * PAIR, PAIR)
        if side == 0:
            to, here, there = slab_at[1], src.at[some, pl.ds(cells - rim, rim)], slo.at[some]
        else:
            to, here, there = slab_at[slabs - 1], src.at[some, pl.ds(0, rim)], shi.at[some]
        return pltpu.make_async_remote_copy(
            src_ref=here, dst_ref=there, send_sem=send_h.at[side, 2 + pair], recv_sem=recv_h.at[side, 2 + pair],
            device_id=(to, group), device_id_type=MESH)

    pairs = fields // PAIR
    has_next, has_prev = slab < slabs - 1, slab > 0

    @pl.when(has_next)
    def _():
        for copy in rim_copies(0):
            copy.start()
        for pair in range(pairs):
            source_copy(0, pair).start()

    @pl.when(has_prev)
    def _():
        for copy in rim_copies(1):
            copy.start()
        for pair in range(pairs):
            source_copy(1, pair).start()

    @pl.when(slab == 0)
    def _():
        cext[0:rim + 1] = jnp.zeros((rim + 1, nz, ny), jnp.float32)
        wext[0:rim] = jnp.zeros((rim, nz, ny), jnp.int32)
        slo[...] = jnp.zeros_like(slo)

    @pl.when(slab == slabs - 1)
    def _():
        cext[rim + 1 + cells:] = jnp.zeros((rim + 1, nz, ny), jnp.float32)
        wext[rim + cells:] = jnp.zeros((rim, nz, ny), jnp.int32)
        shi[...] = jnp.zeros_like(shi)

    def media(e, carry):
        c, fxm = carry
        above = cext[e + 2]
        fxp = harmonic(c, above)
        fyp = jnp.where(yid < ny - 1, harmonic(c, pltpu.roll(c, ny - 1, 1)), 0.0)
        fym = pltpu.roll(fyp, 1, 1)
        fzp = jnp.where(zid < nz - 1, harmonic(c, pltpu.roll(c, nz - 1, 0)), 0.0)
        fzm = pltpu.roll(fzp, 1, 0)
        diagonal_sum = fxp + fxm + fzp + fzm + fyp + fym
        diagonal_sum = diagonal_sum + storage_term + well_conductance * wext[e].astype(jnp.float32)
        inverse = 1.0 / diagonal_sum
        inv[e] = inverse * (poly[-1] / middle)
        gxp[e] = fxp * inverse
        gxm[e] = fxm * inverse
        gzp[e] = fzp * inverse
        gzm[e] = fzm * inverse
        gyp[e] = fyp * inverse
        gym[e] = fym * inverse
        return above, fxp

    def media_planes(low, high):
        lax.fori_loop(low, high, media, (cext[low + 1], harmonic(cext[low], cext[low + 1])))

    media_planes(rim + 1, rim + cells - 1)

    @pl.when(has_prev)
    def _():
        for copy in rim_copies(0):
            copy.wait_recv()

    @pl.when(has_next)
    def _():
        for copy in rim_copies(1):
            copy.wait_recv()

    media_planes(0, rim + 1)
    media_planes(rim + cells - 1, ext)

    @pl.loop(0, fields // PAIR)
    def _(pair):
        first = pair * PAIR

        @pl.when(has_prev)
        def _():
            source_copy(0, pair).wait_recv()

        @pl.when(has_next)
        def _():
            source_copy(1, pair).wait_recv()

        def put(j, e, plane):
            for t in range(tiles):
                v0[j, e, t, inner] = plane[:, t * LANES:(t + 1) * LANES]

        def rim_start(e, unused):
            far = rim + cells + e
            for j in range(PAIR):
                put(j, e, slo[first + j, e].astype(jnp.float32) * inv[e])
                put(j, far, shi[first + j, e].astype(jnp.float32) * inv[far])
            return unused

        def own_start(x, unused):
            own = inv[x + rim]
            for j in range(PAIR):
                put(j, x + rim, src[first + j, x].astype(jnp.float32) * own)
            return unused

        lax.fori_loop(0, rim, rim_start, 0)
        lax.fori_loop(0, cells, own_start, 0)

        value = v0
        for sweep in range(SWEEPS):
            target = ha if sweep % 2 == 0 else hb
            weight = ratio[SWEEPS - 1 - sweep]

            def step(e, unused, value=value, target=target, weight=weight):
                for j in range(PAIR):
                    mids = [value[j, e, t, inner] for t in range(tiles)]
                    ups = [pltpu.roll(mid, LANES - 1, 1) for mid in mids]
                    downs = [pltpu.roll(mid, 1, 1) for mid in mids]
                    for t in range(tiles):
                        at = pl.ds(t * LANES, LANES)
                        up, down = ups[t], downs[t]
                        if t < tiles - 1:
                            up = jnp.where(lane == LANES - 1, ups[t + 1], up)
                        if t > 0:
                            down = jnp.where(lane == 0, downs[t - 1], down)
                        side = gxp[e, :, at] * value[j, e + 1, t, inner] + gxm[e, :, at] * value[j, e - 1, t, inner]
                        flat = gzp[e, :, at] * value[j, e, t, above] + gzm[e, :, at] * value[j, e, t, below]
                        along = gyp[e, :, at] * up + gym[e, :, at] * down
                        target[j, e, t, inner] = weight * v0[j, e, t, inner] + side + (flat + along)
                return unused

            lax.fori_loop(sweep + 1, ext - sweep - 1, step, 0, unroll=UNROLL)
            value = target

        for j in range(PAIR):
            for xb in range(cells // ZB):
                def gather(x, sums, j=j, xb=xb, value=value):
                    plane = xb * ZB + x
                    head = jnp.concatenate([value[j, plane + rim, t, inner] for t in range(tiles)], axis=1)
                    grown = []
                    for k in range(nbz * 3):
                        part = head * md[plane, k]
                        both = part[0:ZB]
                        for half in range(1, nbz):
                            both = both + part[half * ZB:(half + 1) * ZB]
                        grown.append(sums[k] + both)
                    return tuple(grown)

                zero = jnp.zeros((ZB, ny), jnp.float32)
                sums = lax.fori_loop(0, ZB, gather, (zero,) * (nbz * 3), unroll=4)
                for k in range(nbz * 3):
                    red[xb, k, pl.ds(first + j, 1)] = jnp.sum(sums[k], axis=0, keepdims=True)

    ypos = lax.broadcasted_iota(jnp.int32, (ny, nby), 0) // ZB
    bpos = lax.broadcasted_iota(jnp.int32, (ny, nby), 1)
    table = jnp.concatenate([(ypos + dy - 1 == bpos).astype(jnp.float32) for dy in range(3)], axis=0)
    per = nby // rows
    wide = jnp.concatenate([
        jnp.concatenate([red[xb, bz * 3 + dy] for dy in range(3)], axis=1)
        for xb in range(cells // ZB) for bz in range(nbz)
    ], axis=0)
    grad = jnp.dot(wide, table, precision=HIGH, preferred_element_type=jnp.float32)
    for at in range(groups):
        block, part = at // per, at % per
        pieces[at] = grad[block * fields:(block + 1) * fields, part * rows:(part + 1) * rows]

    @pl.when(has_next)
    def _():
        for copy in rim_copies(0):
            copy.wait_send()
        for pair in range(pairs):
            source_copy(0, pair).wait_send()

    @pl.when(has_prev)
    def _():
        for copy in rim_copies(1):
            copy.wait_send()
        for pair in range(pairs):
            source_copy(1, pair).wait_send()

    def piece_copy(d):
        return pltpu.make_async_remote_copy(
            src_ref=pieces.at[group_at[d]], dst_ref=landed.at[group], send_sem=send_a.at[d],
            recv_sem=recv_a.at[d], device_id=(slab, group_at[d]), device_id_type=MESH)

    for d in range(1, groups):
        piece_copy(d).start()
    landed[group] = pieces[group]
    column = lax.broadcasted_iota(jnp.int32, sketch.shape, 1)
    active = jnp.zeros(sketch.shape, jnp.bool_)
    for g in range(groups):
        start = g * fields
        active = active | ((column >= start) & (column < start + counts[g]) & (column < start + fields))
    chosen = jnp.where(active, sketch[...], 0.0)
    for d in range(1, groups):
        piece_copy(d).wait()

    every = landed[...].reshape(groups * fields, rows)
    panel = jnp.dot(chosen, every, precision=HIGH, preferred_element_type=jnp.float32)
    gram = lax.dot_general(panel, panel, (((1,), (1,)), ((), ())), precision=HIGH,
                           preferred_element_type=jnp.float32)
    mine[...] = gram

    def gram_copy(s, g):
        return pltpu.make_async_remote_copy(
            src_ref=mine, dst_ref=grams.at[me], send_sem=send_b.at[s * groups + g],
            recv_sem=recv_b.at[s * groups + g], device_id=(slab_at[s], group_at[g]), device_id_type=MESH)

    for s, g in others:
        gram_copy(s, g).start()
    grams[me] = gram
    for s, g in others:
        gram_copy(s, g).wait()
    upper = jnp.sum(grams[...], axis=0)

    rid = lax.broadcasted_iota(jnp.int32, (rank, 1), 0)
    right = panel
    for j in range(rank - 1):
        column = jnp.where(rid > j, upper[:, j:j + 1] * (1.0 / upper[j:j + 1, j:j + 1]), 0.0)
        right = right - column * right[j:j + 1, :]
        upper = upper - column * upper[j:j + 1, :]
    full = lax.broadcasted_iota(jnp.int32, (rank, rank), 0)
    cid = lax.broadcasted_iota(jnp.int32, (rank, rank), 1)
    pivots = jnp.sum(jnp.where(cid == full, upper, 0.0), axis=1, keepdims=True)
    grow = 1.0 / jnp.sqrt(pivots)
    factor[...] = jnp.where(cid >= full, upper * grow, 0.0) / root
    basis[...] = right * grow * root


def shards(sources, conductivity, well_mask, zone_map, forward_drive, group_counts, sketch):
    fields, cells, nz, ny = sources.shape
    groups = lax.axis_size("probe")
    slabs = lax.axis_size("slab")
    rank = sketch.shape[0]
    rim = SWEEPS
    ext = cells + 2 * rim
    nbz, nby = nz // ZB, ny // ZB
    zone_count = cells // ZB * nbz * nby
    rows = zone_count // groups
    root = math.sqrt(zone_count * slabs)
    count = slabs * groups
    vmem = pl.BlockSpec(memory_space=VMEM)
    plane = (nz, ny)
    f32 = jnp.float32
    dma = pltpu.SemaphoreType.DMA
    basis, factor = pl.pallas_call(
        functools.partial(whole_kernel, root, slabs, groups),
        out_shape=(jax.ShapeDtypeStruct((rank, rows), f32), jax.ShapeDtypeStruct((rank, rank), f32)),
        in_specs=[vmem] * 5 + [pl.BlockSpec(memory_space=pltpu.SMEM), vmem],
        out_specs=(vmem, vmem),
        scratch_shapes=[
            VMEM((fields, rim) + plane, sources.dtype),
            VMEM((fields, rim) + plane, sources.dtype),
            VMEM((ext + 2,) + plane, f32),
            VMEM((ext,) + plane, jnp.int32),
        ] + [VMEM((ext,) + plane, f32)] * 7 + [
            VMEM((cells, nbz * 3) + plane, f32),
        ] + [VMEM((PAIR, ext, ny // LANES, nz + 2 * ZB, LANES), f32)] * 3 + [
            VMEM((cells // ZB, nbz * 3, fields, ny), f32),
            VMEM((groups, fields, rows), f32),
            VMEM((groups, fields, rows), f32),
            VMEM((rank, rank), f32),
            VMEM((count, rank, rank), f32),
            dma((2, 2 + fields // PAIR)), dma((2, 2 + fields // PAIR)), dma((groups,)), dma((groups,)), dma((count,)), dma((count,)),
        ],
        compiler_params=pltpu.CompilerParams(
            collective_id=0, has_side_effects=True, vmem_limit_bytes=56 << 20),
        name="whole",
    )(sources, conductivity, well_mask, zone_map, forward_drive, group_counts, sketch)
    return basis.T, factor


def solution(mesh):
    in_specs = (
        P("probe", "slab", None, None),
        P("slab", None, None),
        P("slab", None, None),
        P("slab", None, None),
        P("slab", None, None),
        P(),
        P(),
    )
    out_specs = (P(("slab", "probe"), None), P())
    return jax.shard_map(shards, mesh=mesh, in_specs=in_specs, out_specs=out_specs, check_vma=False)
```

```python
import functools
import math

import jax
import jax.numpy as jnp
from jax import lax
from jax.experimental import pallas as pl
from jax.experimental.pallas import tpu as pltpu
from jax.sharding import PartitionSpec as P

ZB = 8
SWEEPS = 3
PAIR = 2
UNROLL = 4
LANES = 128

storage_term = 0.2
well_conductance = 4.0
spectrum_low = 0.1
spectrum_high = 2.0

MESH = pl.DeviceIdType.MESH
VMEM = pltpu.VMEM
HIGH = lax.Precision.HIGHEST


def head_polynomial():
    middle = (spectrum_high + spectrum_low) / 2.0
    radius = (spectrum_high - spectrum_low) / 2.0
    aspect = middle / radius
    size = SWEEPS + 1
    update = [1.0] + [0.0] * SWEEPS
    remain = [middle] + [0.0] * SWEEPS
    head = [0.0] * size
    rho_prev = 1.0 / aspect
    for sweep in range(SWEEPS):
        head = [h + u for h, u in zip(head, update)]
        moved = [0.0] + update[:-1]
        remain = [r - u + m for r, u, m in zip(remain, update, moved)]
        rho_new = 1.0 / (2.0 * aspect - rho_prev)
        update = [rho_new * rho_prev * u + 2.0 * rho_new / radius * r for u, r in zip(update, remain)]
        rho_prev = rho_new
    head = [h + u for h, u in zip(head, update)]
    return head, middle


def harmonic(left, right):
    total = left + right
    return 2.0 * left * right / jnp.where(total > 0, total, 1.0)


def whole_kernel(root, slabs, groups, src, cond, well, zone, drive, counts, sketch, basis, factor,
                 slo, shi, cext, wext, inv, gxp, gxm, gzp, gzm, gyp, gym, md, v0, ha, hb, red,
                 pieces, landed, mine, grams, send_h, recv_h, send_a, recv_a, send_b, recv_b):
    fields, cells, nz, ny = src.shape
    rank = sketch.shape[0]
    rows = pieces.shape[2]
    rim = SWEEPS
    ext = cells + 2 * rim
    nbz, nby = nz // ZB, ny // ZB
    poly, middle = head_polynomial()
    ratio = [p / poly[-1] for p in poly]
    yid = lax.broadcasted_iota(jnp.int32, (nz, ny), 1)
    zid = lax.broadcasted_iota(jnp.int32, (nz, ny), 0)

    slab = lax.axis_index("slab")
    group = lax.axis_index("probe")
    me = slab * groups + group
    slab_at = [slab] + [lax.rem(slab + d, slabs) for d in range(1, slabs)]
    group_at = [group] + [lax.rem(group + d, groups) for d in range(1, groups)]
    others = [(s, g) for s in range(slabs) for g in range(groups) if s + g > 0]

    barrier = pltpu.get_barrier_semaphore()
    for s, g in others:
        pl.semaphore_signal(barrier, inc=1, device_id=(slab_at[s], group_at[g]), device_id_type=MESH)

    cext[rim + 1:rim + 1 + cells] = cond[...]
    wext[rim:rim + cells] = well[...]
    scale = float(ZB) ** (-1.5)

    @pl.loop(0, cells)
    def _(x):
        block = (slab * cells + x) // ZB
        rel = zone[x] - block * (nbz * nby) - yid // ZB
        weight = drive[x].astype(jnp.float32) * scale
        for bz in range(nbz):
            for dy in range(3):
                md[x, bz * 3 + dy] = jnp.where(rel == bz * nby + dy - 1, weight, 0.0)

    tiles = ny // LANES
    inner, above, below = pl.ds(ZB, nz), pl.ds(ZB + 1, nz), pl.ds(ZB - 1, nz)
    lane = lax.broadcasted_iota(jnp.int32, (nz, LANES), 1)

    @pl.loop(0, ext)
    def _(e):
        blank = jnp.zeros((ZB, LANES), jnp.float32)
        for buffer in (v0, ha, hb):
            for j in range(PAIR):
                for t in range(tiles):
                    buffer[j, e, t, 0:ZB] = blank
                    buffer[j, e, t, ZB + nz:] = blank

    pl.semaphore_wait(barrier, len(others))

    def rim_copies(side):
        if side == 0:
            to = slab_at[1]
            parts = (
                (cond.at[pl.ds(cells - rim - 1, rim + 1)], cext.at[pl.ds(0, rim + 1)]),
                (well.at[pl.ds(cells - rim, rim)], wext.at[pl.ds(0, rim)]),
            )
        else:
            to = slab_at[slabs - 1]
            parts = (
                (cond.at[pl.ds(0, rim + 1)], cext.at[pl.ds(rim + 1 + cells, rim + 1)]),
                (well.at[pl.ds(0, rim)], wext.at[pl.ds(rim + cells, rim)]),
            )
        return [
            pltpu.make_async_remote_copy(
                src_ref=here, dst_ref=there, send_sem=send_h.at[side, k], recv_sem=recv_h.at[side, k],
                device_id=(to, group), device_id_type=MESH)
            for k, (here, there) in enumerate(parts)
        ]

    def source_copy(side, pair):
        some = pl.ds(pair * PAIR, PAIR)
        if side == 0:
            to, here, there = slab_at[1], src.at[some, pl.ds(cells - rim, rim)], slo.at[some]
        else:
            to, here, there = slab_at[slabs - 1], src.at[some, pl.ds(0, rim)], shi.at[some]
        return pltpu.make_async_remote_copy(
            src_ref=here, dst_ref=there, send_sem=send_h.at[side, 2 + pair], recv_sem=recv_h.at[side, 2 + pair],
            device_id=(to, group), device_id_type=MESH)

    pairs = fields // PAIR
    has_next, has_prev = slab < slabs - 1, slab > 0

    @pl.when(has_next)
    def _():
        for copy in rim_copies(0):
            copy.start()
        for pair in range(pairs):
            source_copy(0, pair).start()

    @pl.when(has_prev)
    def _():
        for copy in rim_copies(1):
            copy.start()
        for pair in range(pairs):
            source_copy(1, pair).start()

    @pl.when(slab == 0)
    def _():
        cext[0:rim + 1] = jnp.zeros((rim + 1, nz, ny), jnp.float32)
        wext[0:rim] = jnp.zeros((rim, nz, ny), jnp.int32)
        slo[...] = jnp.zeros_like(slo)

    @pl.when(slab == slabs - 1)
    def _():
        cext[rim + 1 + cells:] = jnp.zeros((rim + 1, nz, ny), jnp.float32)
        wext[rim + cells:] = jnp.zeros((rim, nz, ny), jnp.int32)
        shi[...] = jnp.zeros_like(shi)

    def media(e, carry):
        c, fxm = carry
        above = cext[e + 2]
        fxp = harmonic(c, above)
        fyp = jnp.where(yid < ny - 1, harmonic(c, pltpu.roll(c, ny - 1, 1)), 0.0)
        fym = pltpu.roll(fyp, 1, 1)
        fzp = jnp.where(zid < nz - 1, harmonic(c, pltpu.roll(c, nz - 1, 0)), 0.0)
        fzm = pltpu.roll(fzp, 1, 0)
        diagonal_sum = fxp + fxm + fzp + fzm + fyp + fym
        diagonal_sum = diagonal_sum + storage_term + well_conductance * wext[e].astype(jnp.float32)
        inverse = 1.0 / diagonal_sum
        inv[e] = inverse * (poly[-1] / middle)
        gxp[e] = fxp * inverse
        gxm[e] = fxm * inverse
        gzp[e] = fzp * inverse
        gzm[e] = fzm * inverse
        gyp[e] = fyp * inverse
        gym[e] = fym * inverse
        return above, fxp

    def media_planes(low, high):
        lax.fori_loop(low, high, media, (cext[low + 1], harmonic(cext[low], cext[low + 1])))

    media_planes(rim + 1, rim + cells - 1)

    @pl.when(has_prev)
    def _():
        for copy in rim_copies(0):
            copy.wait_recv()

    @pl.when(has_next)
    def _():
        for copy in rim_copies(1):
            copy.wait_recv()

    media_planes(0, rim + 1)
    media_planes(rim + cells - 1, ext)

    @pl.loop(0, fields // PAIR)
    def _(pair):
        first = pair * PAIR

        @pl.when(has_prev)
        def _():
            source_copy(0, pair).wait_recv()

        @pl.when(has_next)
        def _():
            source_copy(1, pair).wait_recv()

        def put(j, e, plane):
            for t in range(tiles):
                v0[j, e, t, inner] = plane[:, t * LANES:(t + 1) * LANES]

        def rim_start(e, unused):
            far = rim + cells + e
            for j in range(PAIR):
                put(j, e, slo[first + j, e].astype(jnp.float32) * inv[e])
                put(j, far, shi[first + j, e].astype(jnp.float32) * inv[far])
            return unused

        def own_start(x, unused):
            own = inv[x + rim]
            for j in range(PAIR):
                put(j, x + rim, src[first + j, x].astype(jnp.float32) * own)
            return unused

        lax.fori_loop(0, rim, rim_start, 0)
        lax.fori_loop(0, cells, own_start, 0, unroll=UNROLL)

        value = v0
        for sweep in range(SWEEPS):
            target = ha if sweep % 2 == 0 else hb
            weight = ratio[SWEEPS - 1 - sweep]

            def step(e, unused, value=value, target=target, weight=weight):
                for j in range(PAIR):
                    mids = [value[j, e, t, inner] for t in range(tiles)]
                    ups = [pltpu.roll(mid, LANES - 1, 1) for mid in mids]
                    downs = [pltpu.roll(mid, 1, 1) for mid in mids]
                    for t in range(tiles):
                        at = pl.ds(t * LANES, LANES)
                        up, down = ups[t], downs[t]
                        if t < tiles - 1:
                            up = jnp.where(lane == LANES - 1, ups[t + 1], up)
                        if t > 0:
                            down = jnp.where(lane == 0, downs[t - 1], down)
                        side = gxp[e, :, at] * value[j, e + 1, t, inner] + gxm[e, :, at] * value[j, e - 1, t, inner]
                        flat = gzp[e, :, at] * value[j, e, t, above] + gzm[e, :, at] * value[j, e, t, below]
                        along = gyp[e, :, at] * up + gym[e, :, at] * down
                        target[j, e, t, inner] = weight * v0[j, e, t, inner] + side + (flat + along)
                return unused

            lax.fori_loop(sweep + 1, ext - sweep - 1, step, 0, unroll=UNROLL)
            value = target

        for j in range(PAIR):
            for xb in range(cells // ZB):
                def gather(x, sums, j=j, xb=xb, value=value):
                    plane = xb * ZB + x
                    head = jnp.concatenate([value[j, plane + rim, t, inner] for t in range(tiles)], axis=1)
                    grown = []
                    for k in range(nbz * 3):
                        part = head * md[plane, k]
                        both = part[0:ZB]
                        for half in range(1, nbz):
                            both = both + part[half * ZB:(half + 1) * ZB]
                        grown.append(sums[k] + both)
                    return tuple(grown)

                zero = jnp.zeros((ZB, ny), jnp.float32)
                sums = lax.fori_loop(0, ZB, gather, (zero,) * (nbz * 3), unroll=ZB)
                for k in range(nbz * 3):
                    red[xb, k, pl.ds(first + j, 1)] = jnp.sum(sums[k], axis=0, keepdims=True)

    ypos = lax.broadcasted_iota(jnp.int32, (ny, nby), 0) // ZB
    bpos = lax.broadcasted_iota(jnp.int32, (ny, nby), 1)
    table = jnp.concatenate([(ypos + dy - 1 == bpos).astype(jnp.float32) for dy in range(3)], axis=0)
    per = nby // rows
    wide = jnp.concatenate([
        jnp.concatenate([red[xb, bz * 3 + dy] for dy in range(3)], axis=1)
        for xb in range(cells // ZB) for bz in range(nbz)
    ], axis=0)
    grad = jnp.dot(wide, table, precision=HIGH, preferred_element_type=jnp.float32)
    for at in range(groups):
        block, part = at // per, at % per
        pieces[at] = grad[block * fields:(block + 1) * fields, part * rows:(part + 1) * rows]

    @pl.when(has_next)
    def _():
        for copy in rim_copies(0):
            copy.wait_send()
        for pair in range(pairs):
            source_copy(0, pair).wait_send()

    @pl.when(has_prev)
    def _():
        for copy in rim_copies(1):
            copy.wait_send()
        for pair in range(pairs):
            source_copy(1, pair).wait_send()

    def piece_copy(d):
        return pltpu.make_async_remote_copy(
            src_ref=pieces.at[group_at[d]], dst_ref=landed.at[group], send_sem=send_a.at[d],
            recv_sem=recv_a.at[d], device_id=(slab, group_at[d]), device_id_type=MESH)

    for d in range(1, groups):
        piece_copy(d).start()
    landed[group] = pieces[group]
    column = lax.broadcasted_iota(jnp.int32, sketch.shape, 1)
    active = jnp.zeros(sketch.shape, jnp.bool_)
    for g in range(groups):
        start = g * fields
        active = active | ((column >= start) & (column < start + counts[g]) & (column < start + fields))
    chosen = jnp.where(active, sketch[...], 0.0)
    for d in range(1, groups):
        piece_copy(d).wait()

    every = landed[...].reshape(groups * fields, rows)
    panel = jnp.dot(chosen, every, precision=HIGH, preferred_element_type=jnp.float32)
    gram = lax.dot_general(panel, panel, (((1,), (1,)), ((), ())), precision=HIGH,
                           preferred_element_type=jnp.float32)
    mine[...] = gram

    def gram_copy(s, g):
        return pltpu.make_async_remote_copy(
            src_ref=mine, dst_ref=grams.at[me], send_sem=send_b.at[s * groups + g],
            recv_sem=recv_b.at[s * groups + g], device_id=(slab_at[s], group_at[g]), device_id_type=MESH)

    for s, g in others:
        gram_copy(s, g).start()
    grams[me] = gram
    for s, g in others:
        gram_copy(s, g).wait()
    upper = jnp.sum(grams[...], axis=0)

    rid = lax.broadcasted_iota(jnp.int32, (rank, 1), 0)
    right = panel
    for j in range(rank - 1):
        column = jnp.where(rid > j, upper[:, j:j + 1] * (1.0 / upper[j:j + 1, j:j + 1]), 0.0)
        right = right - column * right[j:j + 1, :]
        upper = upper - column * upper[j:j + 1, :]
    full = lax.broadcasted_iota(jnp.int32, (rank, rank), 0)
    cid = lax.broadcasted_iota(jnp.int32, (rank, rank), 1)
    pivots = jnp.sum(jnp.where(cid == full, upper, 0.0), axis=1, keepdims=True)
    grow = 1.0 / jnp.sqrt(pivots)
    factor[...] = jnp.where(cid >= full, upper * grow, 0.0) / root
    basis[...] = right * grow * root


def shards(sources, conductivity, well_mask, zone_map, forward_drive, group_counts, sketch):
    fields, cells, nz, ny = sources.shape
    groups = lax.axis_size("probe")
    slabs = lax.axis_size("slab")
    rank = sketch.shape[0]
    rim = SWEEPS
    ext = cells + 2 * rim
    nbz, nby = nz // ZB, ny // ZB
    zone_count = cells // ZB * nbz * nby
    rows = zone_count // groups
    root = math.sqrt(zone_count * slabs)
    count = slabs * groups
    vmem = pl.BlockSpec(memory_space=VMEM)
    plane = (nz, ny)
    f32 = jnp.float32
    dma = pltpu.SemaphoreType.DMA
    basis, factor = pl.pallas_call(
        functools.partial(whole_kernel, root, slabs, groups),
        out_shape=(jax.ShapeDtypeStruct((rank, rows), f32), jax.ShapeDtypeStruct((rank, rank), f32)),
        in_specs=[vmem] * 5 + [pl.BlockSpec(memory_space=pltpu.SMEM), vmem],
        out_specs=(vmem, vmem),
        scratch_shapes=[
            VMEM((fields, rim) + plane, sources.dtype),
            VMEM((fields, rim) + plane, sources.dtype),
            VMEM((ext + 2,) + plane, f32),
            VMEM((ext,) + plane, jnp.int32),
        ] + [VMEM((ext,) + plane, f32)] * 7 + [
            VMEM((cells, nbz * 3) + plane, f32),
        ] + [VMEM((PAIR, ext, ny // LANES, nz + 2 * ZB, LANES), f32)] * 3 + [
            VMEM((cells // ZB, nbz * 3, fields, ny), f32),
            VMEM((groups, fields, rows), f32),
            VMEM((groups, fields, rows), f32),
            VMEM((rank, rank), f32),
            VMEM((count, rank, rank), f32),
            dma((2, 2 + fields // PAIR)), dma((2, 2 + fields // PAIR)), dma((groups,)), dma((groups,)), dma((count,)), dma((count,)),
        ],
        compiler_params=pltpu.CompilerParams(
            collective_id=0, has_side_effects=True, vmem_limit_bytes=56 << 20),
        name="whole",
    )(sources, conductivity, well_mask, zone_map, forward_drive, group_counts, sketch)
    return basis.T, factor


def solution(mesh):
    in_specs = (
        P("probe", "slab", None, None),
        P("slab", None, None),
        P("slab", None, None),
        P("slab", None, None),
        P("slab", None, None),
        P(),
        P(),
    )
    out_specs = (P(("slab", "probe"), None), P())
    return jax.shard_map(shards, mesh=mesh, in_specs=in_specs, out_specs=out_specs, check_vma=False)
```
